128 devices in a mesh: tm: 8 (over x, core), dom: 16 (over z, y).
Axes of the slice: x: 4, y: 4, z: 4, core: 2. Of those that a mesh axis runs over, the one named last changes fastest.
Arguments:
- features: bfloat16 [16, 8192, 128], P('tm', 'dom'), may hold values from -6 to 6
- tile_values: bfloat16 [16, 64, 16, 4, 128, 128], P('tm', 'dom'), may hold values from -0.09375 to 0.09375
- tile_cols: int32 [16, 64, 16, 4], P('tm', 'dom'), may hold values from 0 to 3
- tile_count: int32 [16, 64, 16], P('tm', 'dom'), may hold values from 0 to 4, as said below
- hidden_start: float32 [8192, 512], P('dom'), may hold values from -4 to 4
- w_graph: bfloat16 [128, 512], replicated, may hold values from -0.5 to 0.5
- w_input: bfloat16 [512, 1536], replicated, may hold values from -0.25 to 0.25
- w_hidden: bfloat16 [512, 1536], replicated, may hold values from -0.25 to 0.25
- update_bias: float32 [512], replicated, may hold values from -1 to 4
Outputs:
- hidden_seq: bfloat16 [16, 8192, 512], P('tm', 'dom')
The draws below stay inside these ranges and needn't reach their ends.
Inputs may be any that keep to these rules, and one draw needn't show every extreme that they name: `tile_count`: number of live slots; for each row block the entry of its own partition is 4.
All inputs are finite; a program needn't handle non-finite values.
Results may differ from the reference program's by a relative error of at most 0.0052.
Values may be sent and summed in bfloat16 or wider, within the bound.
A program may use at most 128 MiB of HBM per device.

```python
import jax
import jax.numpy as jnp
from jax import lax

H = 512
F = 128
BLK = 128
KP = 4
SNAPS = 16
NODES = 8192
NB_DEV = 4
NBLK = 64
N_DOM = 16


def draw_tile_count(key, part):
    base = jax.random.randint(key, (SNAPS, NBLK, N_DOM), 0, KP + 1)
    owner = (jnp.arange(NBLK, dtype=jnp.int32) // NB_DEV)[None, :, None]
    source = jnp.arange(N_DOM, dtype=jnp.int32)[None, None, :]
    return jnp.where(owner == source, KP, base).astype(jnp.int32)


def with_ends(array, key, smallest, top_value):
    longest = array.shape.index(max(array.shape))
    spots = []
    for shift in (0, 1):
        where = [jax.random.randint(jax.random.fold_in(key, axis), (), 0, length) for axis, length in enumerate(array.shape)]
        where[longest] = (where[longest] + shift) % array.shape[longest]
        spots.append(tuple(where))
    return array.at[spots[0]].set(smallest).at[spots[1]].set(top_value)


def levels(key, dims, cuts, smallest, high):
    def one(position, shards_of):
        heights = jax.random.uniform(jax.random.fold_in(jax.random.fold_in(key, 6), position), (shards_of,), jnp.float32, smallest / len(cuts), high / len(cuts))
        return jnp.repeat(jnp.exp(heights), dims[position] // shards_of).reshape((-1,) + (1,) * (len(dims) - position - 1))

    gain = one(*cuts[0])
    for cut in cuts[1:]:
        gain = gain * one(*cut)
    return gain


def scatter_about(own_key, extent, scale, most, cuts=(), kind=jnp.bfloat16):
    entries = jax.random.normal(own_key, extent, jnp.float32) * scale
    if len(cuts) > 0:
        entries = levels(own_key, extent, cuts, -0.22, 0.18) * entries
    return jnp.clip(entries, min=-most, max=most).astype(kind)


def setup_inputs(seed: int = 0) -> dict:
    seeds = jax.random.split(jax.random.key(seed), 10)
    return {
        "features": scatter_about(seeds[0], (SNAPS, NODES, F), 1.0, 6.0, ((0, 8), (1, 16))),
        "tile_values": scatter_about(seeds[1], (SNAPS, NBLK, N_DOM, KP, BLK, BLK), (BLK * KP * N_DOM // 2) ** -0.5, 0.09375, ((0, 8), (1, 16))),
        "tile_cols": with_ends(jax.random.randint(seeds[2], (SNAPS, NBLK, N_DOM, KP), 0, NB_DEV), jax.random.fold_in(seeds[2], 1), 0, NB_DEV - 1).astype(jnp.int32),
        "tile_count": draw_tile_count(jax.random.fold_in(seeds[9], 71), 0),
        "hidden_start": scatter_about(seeds[4], (NODES, H), 0.7, 4.0, ((0, 16),), jnp.float32),
        "w_graph": scatter_about(seeds[5], (F, H), F ** -0.5, 0.5),
        "w_input": scatter_about(seeds[6], (H, 3 * H), H ** -0.5, 0.25),
        "w_hidden": scatter_about(seeds[7], (H, 3 * H), H ** -0.5, 0.25),
        "update_bias": jnp.clip(jax.random.uniform(seeds[8], (H,), jnp.float32, -1.0, 4.0), -1.0, 4.0),
    }


def propagate_one(projected, tiles, cols, counts):
    blocks = projected.reshape(NBLK, BLK, H)
    offsets = (jnp.arange(N_DOM, dtype=jnp.int32) * NB_DEV)[:, None]
    slots = jnp.arange(KP, dtype=jnp.int32)[None, :]

    def row_block(args):
        tile_row, col_row, count_row = args
        picked = blocks[(col_row + offsets).astype(jnp.int32)].astype(jnp.float32)
        live = (slots < count_row[:, None]).astype(jnp.float32)
        weighted = tile_row.astype(jnp.float32) * live[:, :, None, None]
        return jnp.einsum("pkij,pkjh->ih", weighted, picked)

    out = lax.map(row_block, (tiles, cols, counts))
    return out.reshape(NODES, H)


def reference(features, tile_values, tile_cols, tile_count, hidden_start, w_graph, w_input, w_hidden, update_bias):
    def graph_step(args):
        feats, tiles, cols, counts = args
        projected = jnp.dot(feats, w_graph, preferred_element_type=jnp.float32).astype(jnp.bfloat16)
        propagated = propagate_one(projected, tiles, cols, counts)
        return jax.nn.relu(propagated).astype(jnp.bfloat16)

    graph_out = lax.map(graph_step, (features, tile_values, tile_cols, tile_count))

    def cell(state, graph_row):
        gx = jnp.dot(graph_row, w_input, preferred_element_type=jnp.float32)
        gh = jnp.dot(state.astype(jnp.bfloat16), w_hidden, preferred_element_type=jnp.float32)
        reset = jax.nn.sigmoid(gx[:, :H] + gh[:, :H])
        update = jax.nn.sigmoid(gx[:, H:2 * H] + gh[:, H:2 * H] + update_bias)
        cand = jnp.tanh(gx[:, 2 * H:] + reset * gh[:, 2 * H:])
        state = update * state + (1.0 - update) * cand
        return state, state.astype(jnp.bfloat16)

    final_state, hidden_seq = lax.scan(cell, hidden_start.astype(jnp.float32), graph_out)
    return hidden_seq
```

```python
import functools

import jax
import jax.numpy as jnp
from jax import lax
from jax.experimental import pallas as pl
from jax.experimental.pallas import tpu as pltpu
from jax.sharding import PartitionSpec as P

MESH = pl.DeviceIdType.MESH
SIDE = 4
BF = jnp.bfloat16
F32 = jnp.float32


ORDER = (
    "P0", "Q0", "P1", "E10", "E1b0", "E30", "E20", "E40", "U40", "U20", "E50", "E11",
    "U000", "E60", "E1b1", "U50", "F30", "Q1", "F00", "U60", "U70", "F10", "U80", "E31",
    "F20", "U90", "X0", "E41", "U001", "U41", "E51", "U51", "G10", "G20", "E21", "U21",
    "E61", "G30", "F31", "U71", "J0", "F11", "U81", "F01", "U61", "F21", "U91", "X1",
)
UNITS = {
    "U00": ((0, 0),),
    "U2": ((0, 3), (0, 1), (3, 0), (1, 0)),
    "U4": ((3, 3),),
    "U5": ((1, 3), (3, 1), (1, 1)),
    "U6": ((0, 2), (2, 0)),
    "U7": ((2, 3), (3, 2)),
    "U8": ((2, 1), (1, 2)),
    "U9": ((2, 2),),
}


def kernel(tms, feat, tiles, cols_in, cnt_in, h0, wg, wi, wh, bias, out, *scratch):
    nslot = SIDE * SIDE
    xs = [scratch[s * nslot : (s + 1) * nslot] for s in range(2)]
    (
        tbuf, acc, ax, mine, halves, gx, gx_own, state, state_own, stage, moved, stage_own,
        wgv, wiv, whv, biasv, biasg, graph, cols, cnt,
        ring_send, ring_recv, tile_sem, load_sem, ax_send, ax_recv, half_send, half_recv,
        move_send, move_recv, out_send, out_recv, out_local,
    ) = scratch[2 * nslot :]
    nb = feat.shape[1]
    half = nb // 2
    blk = feat.shape[2]
    kp = tiles.shape[3]
    hid = wg.shape[1]
    share = state.shape[0]
    hs = tms // 2
    wide = hs * share

    me = lax.axis_index("tm")
    dom = lax.axis_index("dom")
    core = me % 2
    chip = me // 2
    partner = me + 1 - 2 * core
    z = dom // SIDE
    y = dom % SIDE

    def at(dz, dy):
        return ((z + dz) % SIDE) * SIDE + (y + dy) % SIDE

    barrier = pltpu.get_barrier_semaphore()
    for dz, dy in ((0, 1), (0, SIDE - 1), (1, 0), (SIDE - 1, 0)):
        pl.semaphore_signal(barrier, inc=1, device_id=(me, at(dz, dy)), device_id_type=MESH)
    for o in range(1, tms):
        pl.semaphore_signal(barrier, inc=1, device_id=((me + o) % tms, dom), device_id_type=MESH)

    own = [pltpu.make_async_copy(feat.at[s], xs[s][0].at[pl.ds(0, nb)], load_sem.at[s]) for s in range(2)]
    loads = [
        pltpu.make_async_copy(wg, wgv, load_sem.at[2]),
        pltpu.make_async_copy(wi, wiv, load_sem.at[3]),
        pltpu.make_async_copy(wh, whv, load_sem.at[4]),
        pltpu.make_async_copy(bias, biasv, load_sem.at[5]),
        pltpu.make_async_copy(h0.at[pl.ds(me * share, share)], state, load_sem.at[6]),
    ]
    own.append(pltpu.make_async_copy(cols_in, cols, load_sem.at[7]))
    own.append(pltpu.make_async_copy(cnt_in, cnt, load_sem.at[8]))
    for c in own:
        c.start()

    def tile_copy(slot):
        return pltpu.make_async_copy(
            tiles.at[:, :, at(slot // SIDE, slot % SIDE)], tbuf.at[slot], tile_sem.at[slot]
        )

    pl.semaphore_wait(barrier, 3 + tms)

    def slot_of(h, df, dg):
        return dg * SIDE + df if h == 0 else df * SIDE + dg

    def to(h, first, way):
        step = 1 if way == 0 else SIDE - 1
        along_y = first == (h == 0)
        return at(0, step) if along_y else at(step, 0)

    def ring(s, h, ident, src, dst_slot, lo, n, target):
        i = (s * 2 + h) * 20 + ident
        return pltpu.make_async_remote_copy(
            src_ref=src,
            dst_ref=xs[s][dst_slot].at[pl.ds(lo, n)],
            send_sem=ring_send.at[i],
            recv_sem=ring_recv.at[i],
            device_id=(me, target),
            device_id_type=MESH,
        )

    def held(s, slot, lo, n):
        return xs[s][slot].at[pl.ds(lo, n)]

    copies = []
    far = (SIDE - 1, 1)
    p1, p1f, p2, p2f = {}, {}, {}, {}
    for s in range(2):
        for h in range(2):
            lo = h * half
            mid = (lo, lo + half // 2)
            for way in range(2):
                first, second = to(h, True, way), to(h, False, way)
                src = feat.at[s, pl.ds(lo, half)]
                p1[s, h, way] = ring(s, h, way, src, slot_of(h, far[way], 0), lo, half, first)
                p1f[s, h, way] = ring(
                    s, h, 2 + way, held(s, slot_of(h, far[way], 0), mid[way], half // 2),
                    slot_of(h, 2, 0), mid[way], half // 2, first,
                )
                for df in range(SIDE):
                    src = feat.at[s, pl.ds(lo, half)] if df == 0 else held(s, slot_of(h, df, 0), lo, half)
                    p2[s, h, df, way] = ring(
                        s, h, 4 + 2 * df + way, src, slot_of(h, df, far[way]), lo, half, second
                    )
                    p2f[s, h, df, way] = ring(
                        s, h, 12 + 2 * df + way, held(s, slot_of(h, df, far[way]), mid[way], half // 2),
                        slot_of(h, df, 2), mid[way], half // 2, second,
                    )
    both = [(h, w) for w in range(2) for h in range(2)]

    def start(table, s, *df):
        for h, w in both:
            c = table[(s, h) + df + (w,)]
            c.start()
            copies.append(c)

    def arrived(table, s, *df):
        for h, w in both:
            table[(s, h) + df + (w,)].wait_recv()

    early = {"P": lambda s: start(p1, s), "Q": lambda s: start(p2, s, 0)}

    def unit(s, *pairs):
        slots = [dz * SIDE + dy for dz, dy in pairs]
        parts = [at(dz, dy) for dz, dy in pairs]
        if s == 0:
            for slot in slots:
                tile_copy(slot).wait()

        def block(r):
            left, right = [], []
            for slot, part in zip(slots, parts):
                n = cnt[s, r, part]
                for k in range(kp):
                    left.append(tbuf[slot, s, r, k])
                    right.append(xs[s][slot][jnp.where(k < n, cols[s, r, k, part], nb)])
            acc[s, r] += jnp.dot(
                jnp.concatenate(left, axis=1), jnp.concatenate(right, axis=0), preferred_element_type=F32
            )

        def body(i, carry):
            block(2 * i)
            block(2 * i + 1)
            return carry

        lax.fori_loop(0, nb // 2, body, 0)

    peers = [(d, k) for d in (2, 1, hs - 1, 0) for k in range(2) if d + k > 0]

    def peer(d, k):
        return 2 * ((chip + d) % hs) + (core + k) % 2

    def exchange_copies(s):
        return [
            pltpu.make_async_remote_copy(
                src_ref=ax.at[s, peer(d, k)],
                dst_ref=mine.at[s, me],
                send_sem=ax_send.at[s, 2 * d + k],
                recv_sem=ax_recv.at[s, 2 * d + k],
                device_id=(peer(d, k), dom),
                device_id_type=MESH,
            )
            for d, k in peers
        ]

    def half_copy(s):
        return pltpu.make_async_remote_copy(
            src_ref=ax.at[s, pl.ds((1 - core) * hs, hs)],
            dst_ref=halves.at[s, core],
            send_sem=half_send.at[s],
            recv_sem=half_recv.at[s],
            device_id=(partner, dom),
            device_id_type=MESH,
        )

    def exchange(s):
        for r in range(nb):
            v = acc[s, r].astype(BF)
            for q in range(blk // share):
                ax[s, r * (blk // share) + q] = v[q * share : (q + 1) * share]
        half_copy(s).start()
        copies.append(half_copy(s))

        @pl.when(me < tms - 1 - s)
        def _():
            for c in exchange_copies(s):
                c.start()

        mine[s, me] = ax[s, me]
        halves[s, core] = ax[s, pl.ds(core * hs, hs)]

    width = min(256, hid)
    pairs_of = 3 * hid // (2 * width)

    def graph_of(rows):
        rows = rows.reshape(-1, feat.shape[3])
        value = jnp.dot(rows, wgv[...], preferred_element_type=F32)
        graph[: rows.shape[0]] = jnp.maximum(value, 0.0).astype(BF)

    def gates(put, n, lo=0, hi=pairs_of, unroll=False):
        def one(j):
            columns = pl.ds(j * width if unroll else pl.multiple_of(j * width, width), width)
            value = jnp.dot(graph[:n], wiv[:, columns], preferred_element_type=F32)
            put(columns, value + biasg[:, columns])

        def body(j, carry):
            one(2 * j)
            one(2 * j + 1)
            return carry

        if unroll:
            for j in range(lo, hi):
                body(j, 0)
        else:
            lax.fori_loop(lo, hi, body, 0)

    def chain_gates(s, lo=0, hi=pairs_of):
        if lo == 0:
            for (d, k), c in zip(peers, exchange_copies(s)):
                @pl.when(peer(hs - d, k) < tms - 1 - s)
                def _(c=c):
                    c.wait_recv()
            graph_of(mine[s, : tms - 1 - s])

        def put(columns, value):
            gx[s, : (tms - 1 - s) * share, columns] = value

        gates(put, (tms - 1 - s) * share, lo, hi, unroll=s == 1)

    def own_gates(first, n):
        def put(columns, value):
            gx_own[first : first + n, columns] = value

        gates(put, n)

    def scale_weights():
        rows = hid // 16

        def body(i, carry):
            r = pl.ds(pl.multiple_of(i * rows, rows), rows)
            whv[r] = whv[r] * 0.5
            wiv[r, : 2 * hid] = wiv[r, : 2 * hid] * 0.5
            return carry

        lax.fori_loop(0, 16, body, 0)
        biasg[...] = jnp.zeros_like(biasg)
        biasg[:, hid : 2 * hid] = biasv[...] * 0.5

    def cell(now, st, gates_at, put, done=None):
        n = now.shape[0]
        for j in range(hid // width):
            c = slice(j * width, (j + 1) * width)

            def gate(g):
                col = slice(g * hid + j * width, g * hid + (j + 1) * width)
                return col, jnp.dot(now, whv[:, col], preferred_element_type=F32)

            col_r, gh_r = gate(0)
            col_c, gh_c = gate(2)
            col_u, gh_u = gate(1)
            for q in range(n // share):
                rows = slice(q * share, (q + 1) * share)
                reset = jnp.tanh(gates_at(rows, col_r) + gh_r[rows])
                part = gh_c[rows]
                cand = jnp.tanh(gates_at(rows, col_c) + (part + reset * part))
                update = jnp.tanh(gates_at(rows, col_u) + gh_u[rows])
                diff = 0.5 * (st[rows, c] - cand)
                new = (cand + diff) + update * diff
                st[rows, c] = new
                put(rows, c, new.astype(BF))
        if done is not None:
            done()


    def move_copy(q):
        return pltpu.make_async_remote_copy(
            src_ref=stage.at[q],
            dst_ref=moved.at[pl.ds((me % hs) * share, share)],
            send_sem=move_send.at[q],
            recv_sem=move_recv.at[me % hs],
            device_id=(2 * q + me // hs, dom),
            device_id_type=MESH,
        )

    def chain(par, sec, q=None):
        base = pl.multiple_of(sec * share, share)

        def gates_at(rows, col):
            return gx[par, pl.ds(base, share), col]

        def put(rows, c, value):
            if q is not None:
                stage[q, rows, c] = value

        def done():
            target = 2 * q + me // hs

            @pl.when(target == me)
            def _():
                moved[pl.ds(pl.multiple_of((me % hs) * share, share), share)] = stage[q]

            @pl.when(target != me)
            def _():
                move_copy(q).start()

        cell(state[...].astype(BF), state, gates_at, put, None if q is None else done)

    def four(i, carry):
        chain(1, 2 * i)
        chain(0, 2 * i + 1)
        chain(1, 2 * i + 1)
        chain(0, 2 * i + 2, i + 1)
        return carry

    for word in ORDER[:3]:
        early[word[0]](int(word[1]))
    for slot in range(nslot):
        tile_copy(slot).start()
    for c in loads:
        c.start()
    for s in range(2):
        for slot in range(nslot):
            xs[s][slot][nb] = jnp.zeros((blk, feat.shape[3]), BF)
    acc[...] = jnp.zeros_like(acc)
    for c in own:
        c.wait()

    def step(kind, s):
        if kind == "P":
            start(p1, s)
        elif kind == "Q":
            start(p2, s, 0)
        elif kind == "E1":
            arrived(p1, s)
            start(p1f, s)
        elif kind == "E1b":
            start(p2, s, 3)
            start(p2, s, 1)
        elif kind == "E3":
            arrived(p1f, s)
            start(p2, s, 2)
        elif kind[0] == "E":
            d = {"E2": 0, "E4": 3, "E5": 1, "E6": 2}[kind]
            arrived(p2, s, d)
            start(p2f, s, d)
        elif kind[0] == "F":
            arrived(p2f, s, int(kind[1]))
        elif kind == "X":
            exchange(s)
            if s == 0:
                for c in loads:
                    c.wait()
                scale_weights()
        elif kind[0] == "G":
            chain_gates(0, int(kind[1]) - 1, int(kind[1]))
        elif kind == "J":
            half_copy(0).wait_recv()
            graph_of(halves[0, 1])
            own_gates(2 * wide, wide)
        else:
            unit(s, *UNITS[kind])

    for word in ORDER[3:]:
        step(word[:-1], int(word[-1]))
    chain(0, 0, 0)
    chain_gates(1)
    lax.fori_loop(0, hs - 1, four, 0)

    half_copy(1).wait_recv()
    graph_of(halves[1])
    own_gates(0, 2 * wide)
    for k in range(hs):
        @pl.when(core * hs + k != me)
        def _(k=k):
            pltpu.make_async_remote_copy(
                src_ref=stage.at[0],
                dst_ref=moved.at[pl.ds(k * share, share)],
                send_sem=move_send.at[0],
                recv_sem=move_recv.at[k],
                device_id=(partner, dom),
                device_id_type=MESH,
            ).wait_recv()

    def sent_copy(j, src):
        return pltpu.make_async_remote_copy(
            src_ref=src,
            dst_ref=out.at[j % 2, pl.ds(core * wide, wide)],
            send_sem=out_send.at[j],
            recv_sem=out_recv.at[j],
            device_id=(partner, dom),
            device_id_type=MESH,
        )

    def kept_copy(j, src):
        return pltpu.make_async_copy(src, out.at[j % 2, pl.ds(core * wide, wide)], out_local.at[j])

    def deliver(j, src):
        @pl.when(core == j // 2)
        def _():
            kept_copy(j, src).start()

        @pl.when(core != j // 2)
        def _():
            sent_copy(j, src).start()

    deliver(0, moved)
    state_own[...] = moved[...].astype(F32)

    def own_step(j, carry):
        base = pl.multiple_of((2 * (j - 1) % 3) * wide, wide)

        def gates_at(rows, col):
            return gx_own[pl.ds(base + rows.start, share), col]

        def put(rows, c, value):
            stage_own[j - 1, rows, c] = value

        def done():
            deliver(j, stage_own.at[j - 1])

        cell(state_own[...].astype(BF), state_own, gates_at, put, done)
        return carry

    lax.fori_loop(1, 4, own_step, 0)

    for c in copies:
        c.wait_send()
    for s in range(2):
        @pl.when(me < tms - 1 - s)
        def _(s=s):
            for c in exchange_copies(s):
                c.wait_send()
    for q in range(hs):
        @pl.when(2 * q + me // hs != me)
        def _(q=q):
            move_copy(q).wait_send()
    for j in range(4):
        src = moved if j == 0 else stage_own.at[j - 1]

        @pl.when(core == j // 2)
        def _(j=j, src=src):
            kept_copy(j, src).wait()
            sent_copy(j, src).wait_recv()

        @pl.when(core != j // 2)
        def _(j=j, src=src):
            sent_copy(j, src).wait_send()


def per_device(tms, features, tile_values, tile_cols, tile_count, hidden_start, w_graph, w_input, w_hidden, update_bias):
    snaps, nodes, feats = features.shape
    nb, kp, blk = tile_values.shape[1], tile_values.shape[3], tile_values.shape[4]
    hid = w_graph.shape[1]
    share = nodes // tms
    nslot = SIDE * SIDE
    hbm = pl.BlockSpec(memory_space=pltpu.HBM)
    dma = pltpu.SemaphoreType.DMA
    scratch = [pltpu.VMEM((nb + 1, blk, feats), BF) for _ in range(2 * nslot)] + [
        pltpu.VMEM((nslot, 2, nb, kp, blk, blk), BF),
        pltpu.VMEM((2, nb, blk, feats), F32),
        pltpu.VMEM((2, tms, share, feats), BF),
        pltpu.VMEM((2, tms, share, feats), BF),
        pltpu.VMEM((2, 2, tms // 2, share, feats), BF),
        pltpu.VMEM((2, tms * share, 3 * hid), F32),
        pltpu.VMEM((3 * nodes // 2, 3 * hid), F32),
        pltpu.VMEM((share, hid), F32),
        pltpu.VMEM((nodes // 2, hid), F32),
        pltpu.VMEM((tms // 2, share, hid), BF),
        pltpu.VMEM((nodes // 2, hid), BF),
        pltpu.VMEM((3, nodes // 2, hid), BF),
        pltpu.VMEM(w_graph.shape, BF),
        pltpu.VMEM(w_input.shape, BF),
        pltpu.VMEM(w_hidden.shape, BF),
        pltpu.VMEM((1, hid), F32),
        pltpu.VMEM((1, 3 * hid), F32),
        pltpu.VMEM((tms * share, hid), BF),
        pltpu.SMEM((2, nb, kp, nslot), jnp.int32),
        pltpu.SMEM((2, nb, nslot), jnp.int32),
        dma((80,)),
        dma((80,)),
        dma((nslot,)),
        dma((9,)),
        dma((2, tms)),
        dma((2, tms)),
        dma((2,)),
        dma((2,)),
        dma((tms // 2,)),
        dma((tms // 2,)),
        dma((4,)),
        dma((4,)),
        dma((4,)),
    ]
    call = pl.pallas_call(
        functools.partial(kernel, tms),
        out_shape=jax.ShapeDtypeStruct((snaps, nodes, hid), BF),
        in_specs=[hbm] * 9,
        out_specs=pl.BlockSpec(memory_space=pl.ANY),
        scratch_shapes=scratch,
        compiler_params=pltpu.CompilerParams(
            collective_id=0, has_side_effects=True, vmem_limit_bytes=44 << 20
        ),
    )
    operands = (
        features.reshape(snaps, nb, blk, feats),
        tile_values,
        tile_cols.transpose(0, 1, 3, 2),
        tile_count,
        hidden_start,
        w_graph,
        w_input,
        w_hidden,
        update_bias.reshape(1, hid),
    )
    return call(*(pltpu.with_memory_space_constraint(v, pltpu.HBM) for v in operands))


def solution(mesh):
    placed = (
        P("tm", "dom", None),
        P("tm", "dom", None, None, None, None),
        P("tm", "dom", None, None),
        P("tm", "dom", None),
        P("dom", None),
        P(),
        P(),
        P(),
        P(),
    )
    return jax.shard_map(
        functools.partial(per_device, mesh.shape["tm"]),
        mesh=mesh,
        in_specs=placed,
        out_specs=P("tm", "dom", None),
        check_vma=False,
    )
```

```python
import functools

import jax
import jax.numpy as jnp
from jax import lax
from jax.experimental import pallas as pl
from jax.experimental.pallas import tpu as pltpu
from jax.sharding import PartitionSpec as P

MESH = pl.DeviceIdType.MESH
SIDE = 4
BF = jnp.bfloat16
F32 = jnp.float32


ORDER = (
    "P0", "Q0", "P1", "E10", "U000", "E1b0", "E20", "E30", "U20", "E11", "E40", "U001", "E50", "U50", "Q1", "E60", "E1b1", "F30", "F00", "F10", "U40", "U80", "E21", "U60", "E31", "U70", "F20", "U90", "X0", "U21", "E41", "U41", "E51", "U51", "F01", "U61", "G10", "E61", "G20", "G30", "F31", "U71", "F11", "J0", "U81", "F21", "U91", "X1",
)
UNITS = {
    "U00": ((0, 0),),
    "U2": ((0, 3), (0, 1), (3, 0), (1, 0)),
    "U4": ((3, 3),),
    "U5": ((1, 3), (3, 1), (1, 1)),
    "U6": ((0, 2), (2, 0)),
    "U7": ((2, 3), (3, 2)),
    "U8": ((2, 1), (1, 2)),
    "U9": ((2, 2),),
}


def kernel(tms, feat, tiles, cols_in, cnt_in, h0, wg, wi, wh, bias, out, *scratch):
    nslot = SIDE * SIDE
    xs = [scratch[s * nslot : (s + 1) * nslot] for s in range(2)]
    (
        tbuf, acc, ax, mine, halves, gx, gx_own, state, state_own, stage, moved, stage_own,
        wgv, wiv, whv, biasv, biasg, graph, cols, cnt,
        ring_send, ring_recv, tile_sem, load_sem, ax_send, ax_recv, half_send, half_recv,
        move_send, move_recv, out_send, out_recv, out_local,
    ) = scratch[2 * nslot :]
    nb = feat.shape[1]
    half = nb // 2
    blk = feat.shape[2]
    kp = tiles.shape[3]
    hid = wg.shape[1]
    share = state.shape[0]
    hs = tms // 2
    wide = hs * share

    me = lax.axis_index("tm")
    dom = lax.axis_index("dom")
    core = me % 2
    chip = me // 2
    partner = me + 1 - 2 * core
    z = dom // SIDE
    y = dom % SIDE

    def at(dz, dy):
        return ((z + dz) % SIDE) * SIDE + (y + dy) % SIDE

    barrier = pltpu.get_barrier_semaphore()
    for dz, dy in ((0, 1), (0, SIDE - 1), (1, 0), (SIDE - 1, 0)):
        pl.semaphore_signal(barrier, inc=1, device_id=(me, at(dz, dy)), device_id_type=MESH)
    for o in range(1, tms):
        pl.semaphore_signal(barrier, inc=1, device_id=((me + o) % tms, dom), device_id_type=MESH)

    own = [pltpu.make_async_copy(feat.at[s], xs[s][0].at[pl.ds(0, nb)], load_sem.at[s]) for s in range(2)]
    loads = [
        pltpu.make_async_copy(wg, wgv, load_sem.at[2]),
        pltpu.make_async_copy(wi, wiv, load_sem.at[3]),
        pltpu.make_async_copy(wh, whv, load_sem.at[4]),
        pltpu.make_async_copy(bias, biasv, load_sem.at[5]),
        pltpu.make_async_copy(h0.at[pl.ds(me * share, share)], state, load_sem.at[6]),
    ]
    own.append(pltpu.make_async_copy(cols_in, cols, load_sem.at[7]))
    own.append(pltpu.make_async_copy(cnt_in, cnt, load_sem.at[8]))
    for c in own:
        c.start()

    def tile_copy(slot):
        return pltpu.make_async_copy(
            tiles.at[:, :, at(slot // SIDE, slot % SIDE)], tbuf.at[slot], tile_sem.at[slot]
        )

    pl.semaphore_wait(barrier, 3 + tms)

    def slot_of(h, df, dg):
        return dg * SIDE + df if h == 0 else df * SIDE + dg

    def to(h, first, way):
        step = 1 if way == 0 else SIDE - 1
        along_y = first == (h == 0)
        return at(0, step) if along_y else at(step, 0)

    def ring(s, h, ident, src, dst_slot, lo, n, target):
        i = (s * 2 + h) * 20 + ident
        return pltpu.make_async_remote_copy(
            src_ref=src,
            dst_ref=xs[s][dst_slot].at[pl.ds(lo, n)],
            send_sem=ring_send.at[i],
            recv_sem=ring_recv.at[i],
            device_id=(me, target),
            device_id_type=MESH,
        )

    def held(s, slot, lo, n):
        return xs[s][slot].at[pl.ds(lo, n)]

    copies = []
    far = (SIDE - 1, 1)
    p1, p1f, p2, p2f = {}, {}, {}, {}
    for s in range(2):
        for h in range(2):
            lo = h * half
            mid = (lo, lo + half // 2)
            for way in range(2):
                first, second = to(h, True, way), to(h, False, way)
                src = feat.at[s, pl.ds(lo, half)]
                p1[s, h, way] = ring(s, h, way, src, slot_of(h, far[way], 0), lo, half, first)
                p1f[s, h, way] = ring(
                    s, h, 2 + way, held(s, slot_of(h, far[way], 0), mid[way], half // 2),
                    slot_of(h, 2, 0), mid[way], half // 2, first,
                )
                for df in range(SIDE):
                    src = feat.at[s, pl.ds(lo, half)] if df == 0 else held(s, slot_of(h, df, 0), lo, half)
                    p2[s, h, df, way] = ring(
                        s, h, 4 + 2 * df + way, src, slot_of(h, df, far[way]), lo, half, second
                    )
                    p2f[s, h, df, way] = ring(
                        s, h, 12 + 2 * df + way, held(s, slot_of(h, df, far[way]), mid[way], half // 2),
                        slot_of(h, df, 2), mid[way], half // 2, second,
                    )
    both = [(h, w) for w in range(2) for h in range(2)]

    def start(table, s, *df):
        for h, w in both:
            c = table[(s, h) + df + (w,)]
            c.start()
            copies.append(c)

    def arrived(table, s, *df):
        for h, w in both:
            table[(s, h) + df + (w,)].wait_recv()

    def relay(table, onward, s, *df):
        for h, w in both:
            table[(s, h) + df + (w,)].wait_recv()
            c = onward[(s, h) + df + (w,)]
            c.start()
            copies.append(c)

    early = {"P": lambda s: start(p1, s), "Q": lambda s: start(p2, s, 0)}

    def unit(s, *pairs):
        slots = [dz * SIDE + dy for dz, dy in pairs]
        parts = [at(dz, dy) for dz, dy in pairs]
        if s == 0:
            for slot in slots:
                tile_copy(slot).wait()

        def block(r):
            left, right = [], []
            for slot, part in zip(slots, parts):
                n = cnt[s, r, part]
                for k in range(kp):
                    left.append(tbuf[slot, s, r, k])
                    right.append(xs[s][slot][jnp.where(k < n, cols[s, r, k, part], nb)])
            acc[s, r] += jnp.dot(
                jnp.concatenate(left, axis=1), jnp.concatenate(right, axis=0), preferred_element_type=F32
            )

        def body(i, carry):
            block(2 * i)
            block(2 * i + 1)
            return carry

        lax.fori_loop(0, nb // 2, body, 0)

    peers = [(d, k) for d in (2, 1, hs - 1, 0) for k in range(2) if d + k > 0]

    def peer(d, k):
        return 2 * ((chip + d) % hs) + (core + k) % 2

    def exchange_copies(s):
        return [
            pltpu.make_async_remote_copy(
                src_ref=ax.at[s, peer(d, k)],
                dst_ref=mine.at[s, me],
                send_sem=ax_send.at[s, 2 * d + k],
                recv_sem=ax_recv.at[s, 2 * d + k],
                device_id=(peer(d, k), dom),
                device_id_type=MESH,
            )
            for d, k in peers
        ]

    def half_copy(s):
        return pltpu.make_async_remote_copy(
            src_ref=ax.at[s, pl.ds((1 - core) * hs, hs)],
            dst_ref=halves.at[s, core],
            send_sem=half_send.at[s],
            recv_sem=half_recv.at[s],
            device_id=(partner, dom),
            device_id_type=MESH,
        )

    def exchange(s):
        for r in range(nb):
            v = acc[s, r].astype(BF)
            for q in range(blk // share):
                ax[s, r * (blk // share) + q] = v[q * share : (q + 1) * share]
        half_copy(s).start()
        copies.append(half_copy(s))

        @pl.when(me < tms - 1 - s)
        def _():
            for c in exchange_copies(s):
                c.start()

        mine[s, me] = ax[s, me]
        halves[s, core] = ax[s, pl.ds(core * hs, hs)]

    width = min(256, hid)
    pairs_of = 3 * hid // (2 * width)

    def graph_of(rows):
        rows = rows.reshape(-1, feat.shape[3])
        value = jnp.dot(rows, wgv[...], preferred_element_type=F32)
        graph[: rows.shape[0]] = jnp.maximum(value, 0.0).astype(BF)

    def gates(put, n, lo=0, hi=pairs_of, unroll=False):
        def one(j):
            columns = pl.ds(j * width if unroll else pl.multiple_of(j * width, width), width)
            value = jnp.dot(graph[:n], wiv[:, columns], preferred_element_type=F32)
            put(columns, value + biasg[:, columns])

        def body(j, carry):
            one(2 * j)
            one(2 * j + 1)
            return carry

        if unroll:
            for j in range(lo, hi):
                body(j, 0)
        else:
            lax.fori_loop(lo, hi, body, 0)

    def chain_gates(s, lo=0, hi=pairs_of):
        if lo == 0:
            for (d, k), c in zip(peers, exchange_copies(s)):
                @pl.when(peer(hs - d, k) < tms - 1 - s)
                def _(c=c):
                    c.wait_recv()
            graph_of(mine[s, : tms - 1 - s])

        def put(columns, value):
            gx[s, : (tms - 1 - s) * share, columns] = value

        gates(put, (tms - 1 - s) * share, lo, hi, unroll=s == 1)

    def own_gates(first, n):
        def put(columns, value):
            gx_own[first : first + n, columns] = value

        gates(put, n)

    def scale_weights():
        rows = hid // 16

        def body(i, carry):
            r = pl.ds(pl.multiple_of(i * rows, rows), rows)
            whv[r] = whv[r] * 0.5
            wiv[r, : 2 * hid] = wiv[r, : 2 * hid] * 0.5
            return carry

        lax.fori_loop(0, 16, body, 0)
        biasg[...] = jnp.zeros_like(biasg)
        biasg[:, hid : 2 * hid] = biasv[...] * 0.5

    def cell(now, st, gates_at, put, done=None):
        n = now.shape[0]
        for j in range(hid // width):
            c = slice(j * width, (j + 1) * width)

            def gate(g):
                col = slice(g * hid + j * width, g * hid + (j + 1) * width)
                return col, jnp.dot(now, whv[:, col], preferred_element_type=F32)

            col_r, gh_r = gate(0)
            col_c, gh_c = gate(2)
            col_u, gh_u = gate(1)
            for q in range(n // share):
                rows = slice(q * share, (q + 1) * share)
                reset = jnp.tanh(gates_at(rows, col_r) + gh_r[rows])
                part = gh_c[rows]
                cand = jnp.tanh(gates_at(rows, col_c) + (part + reset * part))
                update = jnp.tanh(gates_at(rows, col_u) + gh_u[rows])
                diff = 0.5 * (st[rows, c] - cand)
                new = (cand + diff) + update * diff
                st[rows, c] = new
                put(rows, c, new.astype(BF))
        if done is not None:
            done()


    def move_copy(q):
        return pltpu.make_async_remote_copy(
            src_ref=stage.at[q],
            dst_ref=moved.at[pl.ds((me % hs) * share, share)],
            send_sem=move_send.at[q],
            recv_sem=move_recv.at[me % hs],
            device_id=(2 * q + me // hs, dom),
            device_id_type=MESH,
        )

    def chain(par, sec, q=None):
        base = pl.multiple_of(sec * share, share)

        def gates_at(rows, col):
            return gx[par, pl.ds(base, share), col]

        def put(rows, c, value):
            if q is not None:
                stage[q, rows, c] = value

        def done():
            target = 2 * q + me // hs

            @pl.when(target == me)
            def _():
                moved[pl.ds(pl.multiple_of((me % hs) * share, share), share)] = stage[q]

            @pl.when(target != me)
            def _():
                move_copy(q).start()

        cell(state[...].astype(BF), state, gates_at, put, None if q is None else done)

    def four(i, carry):
        chain(1, 2 * i)
        chain(0, 2 * i + 1)
        chain(1, 2 * i + 1)
        chain(0, 2 * i + 2, i + 1)
        return carry

    for word in ORDER[:3]:
        early[word[0]](int(word[1]))
    for slot in range(nslot):
        tile_copy(slot).start()
    for c in loads:
        c.start()
    for s in range(2):
        for slot in range(nslot):
            xs[s][slot][nb] = jnp.zeros((blk, feat.shape[3]), BF)
    acc[...] = jnp.zeros_like(acc)
    for c in own:
        c.wait()

    def step(kind, s):
        if kind == "P":
            start(p1, s)
        elif kind == "Q":
            start(p2, s, 0)
        elif kind == "E1":
            relay(p1, p1f, s)
        elif kind == "E1b":
            start(p2, s, 3)
            start(p2, s, 1)
        elif kind == "E3":
            arrived(p1f, s)
            start(p2, s, 2)
        elif kind[0] == "E":
            d = {"E2": 0, "E4": 3, "E5": 1, "E6": 2}[kind]
            relay(p2, p2f, s, d)
        elif kind[0] == "F":
            arrived(p2f, s, int(kind[1]))
        elif kind == "X":
            exchange(s)
            if s == 0:
                for c in loads:
                    c.wait()
                scale_weights()
        elif kind[0] == "G":
            chain_gates(0, int(kind[1]) - 1, int(kind[1]))
        elif kind == "J":
            half_copy(0).wait_recv()
            graph_of(halves[0, 1])
            own_gates(2 * wide, wide)
        else:
            unit(s, *UNITS[kind])

    for word in ORDER[3:]:
        step(word[:-1], int(word[-1]))
    chain(0, 0, 0)
    chain_gates(1)
    lax.fori_loop(0, hs - 1, four, 0)

    half_copy(1).wait_recv()
    graph_of(halves[1])
    own_gates(0, 2 * wide)
    for k in range(hs):
        @pl.when(core * hs + k != me)
        def _(k=k):
            pltpu.make_async_remote_copy(
                src_ref=stage.at[0],
                dst_ref=moved.at[pl.ds(k * share, share)],
                send_sem=move_send.at[0],
                recv_sem=move_recv.at[k],
                device_id=(partner, dom),
                device_id_type=MESH,
            ).wait_recv()

    def sent_copy(j, src):
        return pltpu.make_async_remote_copy(
            src_ref=src,
            dst_ref=out.at[j % 2, pl.ds(core * wide, wide)],
            send_sem=out_send.at[j],
            recv_sem=out_recv.at[j],
            device_id=(partner, dom),
            device_id_type=MESH,
        )

    def kept_copy(j, src):
        return pltpu.make_async_copy(src, out.at[j % 2, pl.ds(core * wide, wide)], out_local.at[j])

    def deliver(j, src):
        @pl.when(core == j // 2)
        def _():
            kept_copy(j, src).start()

        @pl.when(core != j // 2)
        def _():
            sent_copy(j, src).start()

    deliver(0, moved)
    state_own[...] = moved[...].astype(F32)

    def own_step(j, carry):
        base = pl.multiple_of((2 * (j - 1) % 3) * wide, wide)

        def gates_at(rows, col):
            return gx_own[pl.ds(base + rows.start, share), col]

        def put(rows, c, value):
            stage_own[j - 1, rows, c] = value

        def done():
            deliver(j, stage_own.at[j - 1])

        cell(state_own[...].astype(BF), state_own, gates_at, put, done)
        return carry

    lax.fori_loop(1, 4, own_step, 0)

    for c in copies:
        c.wait_send()
    for s in range(2):
        @pl.when(me < tms - 1 - s)
        def _(s=s):
            for c in exchange_copies(s):
                c.wait_send()
    for q in range(hs):
        @pl.when(2 * q + me // hs != me)
        def _(q=q):
            move_copy(q).wait_send()
    for j in range(4):
        src = moved if j == 0 else stage_own.at[j - 1]

        @pl.when(core == j // 2)
        def _(j=j, src=src):
            kept_copy(j, src).wait()
            sent_copy(j, src).wait_recv()

        @pl.when(core != j // 2)
        def _(j=j, src=src):
            sent_copy(j, src).wait_send()


def per_device(tms, features, tile_values, tile_cols, tile_count, hidden_start, w_graph, w_input, w_hidden, update_bias):
    snaps, nodes, feats = features.shape
    nb, kp, blk = tile_values.shape[1], tile_values.shape[3], tile_values.shape[4]
    hid = w_graph.shape[1]
    share = nodes // tms
    nslot = SIDE * SIDE
    hbm = pl.BlockSpec(memory_space=pltpu.HBM)
    dma = pltpu.SemaphoreType.DMA
    scratch = [pltpu.VMEM((nb + 1, blk, feats), BF) for _ in range(2 * nslot)] + [
        pltpu.VMEM((nslot, 2, nb, kp, blk, blk), BF),
        pltpu.VMEM((2, nb, blk, feats), F32),
        pltpu.VMEM((2, tms, share, feats), BF),
        pltpu.VMEM((2, tms, share, feats), BF),
        pltpu.VMEM((2, 2, tms // 2, share, feats), BF),
        pltpu.VMEM((2, tms * share, 3 * hid), F32),
        pltpu.VMEM((3 * nodes // 2, 3 * hid), F32),
        pltpu.VMEM((share, hid), F32),
        pltpu.VMEM((nodes // 2, hid), F32),
        pltpu.VMEM((tms // 2, share, hid), BF),
        pltpu.VMEM((nodes // 2, hid), BF),
        pltpu.VMEM((3, nodes // 2, hid), BF),
        pltpu.VMEM(w_graph.shape, BF),
        pltpu.VMEM(w_input.shape, BF),
        pltpu.VMEM(w_hidden.shape, BF),
        pltpu.VMEM((1, hid), F32),
        pltpu.VMEM((1, 3 * hid), F32),
        pltpu.VMEM((tms * share, hid), BF),
        pltpu.SMEM((2, nb, kp, nslot), jnp.int32),
        pltpu.SMEM((2, nb, nslot), jnp.int32),
        dma((80,)),
        dma((80,)),
        dma((nslot,)),
        dma((9,)),
        dma((2, tms)),
        dma((2, tms)),
        dma((2,)),
        dma((2,)),
        dma((tms // 2,)),
        dma((tms // 2,)),
        dma((4,)),
        dma((4,)),
        dma((4,)),
    ]
    call = pl.pallas_call(
        functools.partial(kernel, tms),
        out_shape=jax.ShapeDtypeStruct((snaps, nodes, hid), BF),
        in_specs=[hbm] * 9,
        out_specs=pl.BlockSpec(memory_space=pl.ANY),
        scratch_shapes=scratch,
        compiler_params=pltpu.CompilerParams(
            collective_id=0, has_side_effects=True, vmem_limit_bytes=44 << 20
        ),
    )
    operands = (
        features.reshape(snaps, nb, blk, feats),
        tile_values,
        tile_cols.transpose(0, 1, 3, 2),
        tile_count,
        hidden_start,
        w_graph,
        w_input,
        w_hidden,
        update_bias.reshape(1, hid),
    )
    return call(*(pltpu.with_memory_space_constraint(v, pltpu.HBM) for v in operands))


def solution(mesh):
    placed = (
        P("tm", "dom", None),
        P("tm", "dom", None, None, None, None),
        P("tm", "dom", None, None),
        P("tm", "dom", None),
        P("dom", None),
        P(),
        P(),
        P(),
        P(),
    )
    return jax.shard_map(
        functools.partial(per_device, mesh.shape["tm"]),
        mesh=mesh,
        in_specs=placed,
        out_specs=P("tm", "dom", None),
        check_vma=False,
    )
```
